256 devices in a mesh: frame: 64 (over y, z, core), head: 4 (over x).
Axes of the slice: x: 4, y: 4, z: 8, core: 2. Of those that a mesh axis runs over, the one named last changes fastest.
Arguments:
- span_q: bfloat16 [32768, 3072], P(('frame', 'head')), may hold values from -40 to 40
- span_k: bfloat16 [32768, 3072], P(('frame', 'head')), may hold values from -4 to 4
- span_v: bfloat16 [32768, 3072], P(('frame', 'head')), may hold values from -12 to 12
- bank_k: bfloat16 [1536, 32, 3072], P('frame', None, 'head'), may hold values from -4 to 4
- bank_v: bfloat16 [1536, 32, 3072], P('frame', None, 'head'), may hold values from -12 to 12
- frame_slot: int32 [1536], replicated, may hold values from 0 to 1535, as said below
- picks: int32 [64, 64], replicated, may hold values from 0 to 1535, as said below
- counts: int32 [64], replicated, may hold values from 44 to 64, as said below
- out_weight: bfloat16 [3072, 3072], P('head'), may hold values from -0.109375 to 0.109375
Outputs:
- mixed: bfloat16 [32768, 3072], P(('frame', 'head'))
The draws below stay inside these ranges and needn't reach their ends.
Inputs may be any that keep to these rules, and one draw needn't show every extreme that they name: `frame_slot`: A permutation of the frame ids. For every span c the first counts[c] entries of picks[c] are distinct frames; at most 2 of them lie in bank rows j * 24 to (j + 1) * 24 - 1 for any j, and for every span some j holds exactly 2. Entries past counts[c] are frame ids that are not used. `counts`: some span retrieves exactly 64 frames.
All inputs are finite; a program needn't handle non-finite values.
Results may differ from the reference program's by a relative error of at most 0.013.
Values may be sent and summed in bfloat16 or wider, within the bound.
A program may use at most 128 MiB of HBM per device.

```python
import math
import jax
import jax.numpy as jnp
from jax import lax

HEADS = 24
HEAD_DIM = 128
D = 3072
ROWS = 512
MTOK = 32
FD = 24
MAXR = 64
MINR = 44
SPANS = 64
FRAMES = 1536
CAP = 2
N_HEAD = 4


def retrieval(key):
    slot_of = jax.random.permutation(jax.random.fold_in(key, 11), FRAMES).astype(jnp.int32)
    order_keys = jax.random.split(jax.random.fold_in(key, 12), SPANS)
    owner_order = jax.vmap(lambda one: jax.random.permutation(one, SPANS))(order_keys).astype(jnp.int32)
    offsets = jax.random.randint(jax.random.fold_in(key, 13), (SPANS, SPANS), 0, FD).astype(jnp.int32)
    position = jnp.arange(MAXR, dtype=jnp.int32)
    beyond = jnp.maximum(position - CAP, 0)
    which = jnp.where(position < CAP, 0, 1 + beyond % (SPANS - 1))
    level = jnp.where(position < CAP, position, beyond // (SPANS - 1))
    owner = jnp.take_along_axis(owner_order, jnp.broadcast_to(which, (SPANS, MAXR)), axis=1)
    offset = jnp.take_along_axis(offsets, owner, axis=1)
    bank_row = (owner * FD + (offset + level[None, :]) % FD).astype(jnp.int32)
    inverse = jnp.zeros((FRAMES,), jnp.int32).at[slot_of].set(jnp.arange(FRAMES, dtype=jnp.int32))
    chosen = inverse[bank_row].astype(jnp.int32)
    number = jax.random.randint(jax.random.fold_in(key, 14), (SPANS,), MINR, MAXR + 1).astype(jnp.int32)
    forced = jax.random.randint(jax.random.fold_in(key, 15), (), 0, SPANS)
    number = jnp.where(jnp.arange(SPANS) == forced, MAXR, number).astype(jnp.int32)
    return (slot_of, chosen, number)


def draw_frame_slot(key, part):
    return retrieval(key)[0]


def draw_picks(key, part):
    return retrieval(key)[1]


def draw_counts(key, part):
    return retrieval(key)[2]


def draw_bank_k(key, part):
    full = jnp.clip(jax.random.normal(jax.random.fold_in(key, 31), (FRAMES, MTOK, D), jnp.float32), -4.0, 4.0)
    return full.astype(jnp.bfloat16)


def key_rows(key):
    total_rows = SPANS * ROWS
    base = jnp.clip(jax.random.normal(jax.random.fold_in(key, 21), (total_rows, D), jnp.float32), -4.0, 4.0)
    return base


def draw_span_k(key, part):
    return key_rows(key).astype(jnp.bfloat16)


def draw_span_q(key, part):
    total_rows = SPANS * ROWS
    values = jnp.clip(2.5 * jax.random.normal(jax.random.fold_in(key, 22), (total_rows, D), jnp.float32), -15.0, 15.0)
    return values.astype(jnp.bfloat16)


def level_of(key, extent, cuts, smallest, high):
    loudness, own = 1.0, jax.random.fold_in(key, 6)
    for dim, parts in cuts:
        heights = jnp.exp(jax.random.uniform(jax.random.fold_in(own, dim), (parts,), jnp.float32, smallest / len(cuts), high / len(cuts)))
        loudness = loudness * jnp.repeat(heights, extent[dim] // parts).reshape([-1 if axis == dim else 1 for axis in range(len(extent))])
    return loudness


def bell_draw(stream_key, dims, spread, bound, shards=(), kind=jnp.bfloat16):
    loudness = level_of(stream_key, dims, shards, -0.22, 0.18) if shards else 1.0
    values = jax.random.normal(stream_key, dims, jnp.float32) * spread * loudness
    return jnp.minimum(jnp.maximum(values, -bound), bound).astype(kind)


def setup_inputs(seed: int = 0) -> dict:
    arg_keys = jax.random.split(jax.random.key(seed), 10)
    return {
        "span_q": draw_span_q(jax.random.fold_in(arg_keys[9], 71), 0),
        "span_k": draw_span_k(jax.random.fold_in(arg_keys[9], 71), 0),
        "span_v": bell_draw(arg_keys[2], (SPANS * ROWS, D), 2.0, 12.0, ((0, 256),)),
        "bank_k": draw_bank_k(jax.random.fold_in(arg_keys[9], 71), 0),
        "bank_v": bell_draw(arg_keys[4], (FRAMES, MTOK, D), 2.0, 12.0, ((0, 64), (2, 4))),
        "frame_slot": draw_frame_slot(jax.random.fold_in(arg_keys[9], 71), 0),
        "picks": draw_picks(jax.random.fold_in(arg_keys[9], 71), 0),
        "counts": draw_counts(jax.random.fold_in(arg_keys[9], 71), 0),
        "out_weight": bell_draw(arg_keys[8], (D, D), D ** -0.5, 0.109375, ((0, 4),)),
    }


def reference(span_q, span_k, span_v, bank_k, bank_v, frame_slot, picks, counts, out_weight):
    scale = 1.0 / math.sqrt(HEAD_DIM)
    group_width = D // N_HEAD

    def one_span(span):
        start = (span * ROWS).astype(jnp.int32)
        queries = lax.dynamic_slice_in_dim(span_q, start, ROWS, 0).reshape(ROWS, HEADS, HEAD_DIM).astype(jnp.float32)
        own_keys = lax.dynamic_slice_in_dim(span_k, start, ROWS, 0).reshape(ROWS, HEADS, HEAD_DIM)
        own_vals = lax.dynamic_slice_in_dim(span_v, start, ROWS, 0).reshape(ROWS, HEADS, HEAD_DIM)
        listed = lax.dynamic_slice_in_dim(picks, span, 1, 0)[0]
        number = lax.dynamic_slice_in_dim(counts, span, 1, 0)[0]
        live = jnp.arange(MAXR, dtype=jnp.int32) < number
        bank_rows = frame_slot[listed].astype(jnp.int32)
        mem_keys = bank_k[bank_rows].reshape(MAXR * MTOK, HEADS, HEAD_DIM)
        mem_vals = bank_v[bank_rows].reshape(MAXR * MTOK, HEADS, HEAD_DIM)
        keys = jnp.concatenate([own_keys, mem_keys], axis=0).astype(jnp.float32)
        values = jnp.concatenate([own_vals, mem_vals], axis=0).astype(jnp.float32)
        mask = jnp.concatenate([jnp.ones((ROWS,), bool), jnp.repeat(live, MTOK)])
        scores = jnp.einsum('qhd,khd->hqk', queries, keys) * scale
        scores = jnp.where(mask[None, None, :], scores, -1e+30)
        top = lax.optimization_barrier(jnp.max(scores, axis=-1, keepdims=True))
        expo = jnp.exp(scores - top)
        total = lax.optimization_barrier(jnp.sum(expo, axis=-1))
        weights = expo.astype(jnp.bfloat16)
        weights = lax.optimization_barrier(weights).astype(jnp.float32)
        numer = jnp.einsum('hqk,khd->qhd', weights, values)
        attn = (numer / jnp.transpose(total)[:, :, None]).astype(jnp.bfloat16).reshape(ROWS, D)
        mixed = jnp.zeros((ROWS, D), jnp.float32)
        for group in range(N_HEAD):
            lo = group * group_width
            part = jnp.dot(attn[:, lo:lo + group_width], out_weight[lo:lo + group_width], preferred_element_type=jnp.float32)
            part = lax.optimization_barrier(part.astype(jnp.bfloat16))
            mixed = mixed + part.astype(jnp.float32)
        return mixed.astype(jnp.bfloat16)
    result = lax.map(one_span, jnp.arange(SPANS, dtype=jnp.int32))
    return result.reshape(SPANS * ROWS, D)
```

```python
import math

import jax
import jax.numpy as jnp
from jax import lax
from jax.experimental import pallas as pl
from jax.experimental.pallas import tpu as pltpu
from jax.sharding import PartitionSpec as P

HEAD_DIM = 128
NX, NY, NZ, NC = 4, 4, 8, 2
PLANE = NY * NC
PAIRS = 3
NEG = -1e30
MESH = pl.DeviceIdType.MESH


def side_units(step):
    return [u for u in range(4) if (4 if (u // 2 + u % 2) % 2 == 0 else 3) >= step]


def kernel(
    rows_ref, bias_ref, q_ref, k_ref, v_ref, bk_ref, bv_ref, w_ref,
    out_ref, wfull_ref,
    qx, kx, vx, bank0, bank1, bank2, qt, rb, lb, home, hlse, mine,
    xq_s, xq_r, xk_s, xk_r, own_sem, bo_sem, w_own, w_s, w_r, wd_s, wd_r,
    a_s, a_r, b_s, b_r, d_s, d_r, g_s, g_r, o_s, o_r, l_s, l_r, t_s, t_r, t_own,
):
    frame = lax.axis_index("frame")
    x = lax.axis_index("head")
    y, z, c = frame // (NZ * NC), (frame // NC) % NZ, frame % NC
    rows = q_ref.shape[0]
    width = qx.shape[1]
    frames = bk_ref.shape[0]
    half = frames // 2
    wrows = w_ref.shape[0]
    whalf = wrows // 2
    banks = (bank0, bank1, bank2)
    factor = math.log2(math.e) / math.sqrt(HEAD_DIM)

    def dev_y(step):
        return ((((y + step + NY) % NY) * NZ + z) * NC + c, x)

    def dev_z(step):
        return ((y * NZ + (z + step + NZ) % NZ) * NC + c, x)

    def dev_x(step):
        return (frame, (x + step) % NX)

    sibling = ((y * NZ + z) * NC + 1 - c, x)

    def lanes(start, size):
        return pl.ds(pl.multiple_of(start, HEAD_DIM), size)

    def remote(src, dst, s, r, dev):
        return pltpu.make_async_remote_copy(
            src_ref=src, dst_ref=dst, send_sem=s, recv_sem=r, device_id=dev, device_id_type=MESH
        )

    my_rows = pl.ds(pl.multiple_of(x * rows, rows), rows)

    def x_query(p, dx):
        peer = (x + dx) % NX
        return remote(
            q_ref.at[:, lanes(peer * width + p * 256, 256)],
            qx.at[my_rows, pl.ds(p * 256, 256)],
            xq_s.at[p, dx - 1], xq_r.at[p, dx - 1], dev_x(dx),
        )

    def x_keys(kv, dx):
        peer = (x + dx) % NX
        src, dst = ((k_ref, kx), (v_ref, vx))[kv]
        return remote(
            src.at[:, lanes(peer * width, width)], dst.at[my_rows, :],
            xk_s.at[kv, dx - 1], xk_r.at[kv, dx - 1], dev_x(dx),
        )

    def own_rows(i):
        src, dst = ((q_ref, qx), (k_ref, kx), (v_ref, vx))[i]
        return pltpu.make_async_copy(
            src.at[:, lanes(x * width, width)], dst.at[my_rows, :], own_sem.at[i]
        )

    def own_bank(kv, p):
        return pltpu.make_async_copy(
            (bk_ref, bv_ref)[kv].at[:, :, cols(p)], block(kv, y, p), bo_sem.at[p, kv]
        )

    def cols(p):
        return pl.ds(p * 256, 256)

    def block(kv, yy, p):
        return banks[p].at[kv, pl.ds(((yy + NY) % NY * NC + c) * frames, frames)]

    def half_block(kv, yy, which, p):
        start = ((yy + NY) % NY * NC + c) * frames + which * half
        return banks[p].at[kv, pl.ds(start, half)]

    def bank_a(p, kv, d):
        return remote(
            (bk_ref, bv_ref)[kv].at[:, :, cols(p)], block(kv, y, p),
            a_s.at[p, kv, d], a_r.at[p, kv, d], dev_y(1 - 2 * d),
        )

    def bank_b(p, kv, d):
        view = half_block(kv, y - (1 - 2 * d), d, p)
        return remote(view, view, b_s.at[p, kv, d], b_r.at[p, kv, d], dev_y(1 - 2 * d))

    def bank_d(p, kv, t):
        if t == 0:
            src, dst = (bk_ref, bv_ref)[kv].at[:, :, cols(p)], block(kv, y, p)
        elif t <= 2:
            src = dst = block(kv, y - (1 - 2 * (t - 1)), p)
        else:
            src = dst = half_block(kv, y + 2, t - 3, p)
        return remote(src, dst, d_s.at[p, kv, t], d_r.at[p, kv, t], sibling)

    def ag(s, k, h):
        before = 0 if k == 1 else s * 4 + k - 1
        return remote(
            qt.at[before, h], qt.at[s * 4 + k, h], g_s.at[s, k, h], g_r.at[s, k, h], dev_z(2 * s - 1)
        )

    def back(s, k, h):
        return (
            remote(rb.at[s, k, h], rb.at[s, k - 1, h], o_s.at[s, k, h], o_r.at[s, k - 1, h], dev_z(1 - 2 * s)),
            remote(lb.at[s, k, h], lb.at[s, k - 1, h], l_s.at[s, k, h], l_r.at[s, k - 1, h], dev_z(1 - 2 * s)),
        )

    def w_x(dx):
        return remote(
            w_ref.at[pl.ds(c * whalf, whalf)], wfull_ref.at[pl.ds(x * wrows + c * whalf, whalf)],
            w_s.at[dx - 1], w_r.at[dx - 1], dev_x(dx),
        )

    def w_d(dx):
        view = wfull_ref.at[pl.ds((x - dx + NX) % NX * wrows + c * whalf, whalf)]
        return remote(view, view, wd_s.at[dx - 1], wd_r.at[dx - 1], sibling)

    def w_mine():
        return pltpu.make_async_copy(w_ref, wfull_ref.at[pl.ds(x * wrows, wrows)], w_own)

    def attn_x(p, dx):
        peer = (x + dx) % NX
        return remote(
            mine.at[pl.ds(pl.multiple_of(peer * rows, rows), rows), cols(p)],
            out_ref.at[:, lanes(x * width + p * 256, 256)],
            t_s.at[p, dx - 1], t_r.at[p, dx - 1], dev_x(dx),
        )

    def attn_own(p):
        return pltpu.make_async_copy(
            mine.at[my_rows, cols(p)], out_ref.at[:, lanes(x * width + p * 256, 256)], t_own.at[p]
        )

    def softmax(keys, values, queries, biases):
        scores = jnp.dot(keys, queries, preferred_element_type=jnp.float32) * factor
        if biases is not None:
            step = scores.shape[0] // len(biases)
            scores = jnp.concatenate(
                [scores[i * step : (i + 1) * step] + b for i, b in enumerate(biases)], axis=0
            )
        top = jnp.max(scores, axis=0, keepdims=True)
        expo = jnp.exp2(scores - top)
        total = jnp.sum(expo, axis=0, keepdims=True)
        numer = lax.dot_general(
            values, expo.astype(jnp.bfloat16), (((0,), (0,)), ((), ())),
            preferred_element_type=jnp.float32,
        )
        return numer / total, top + jnp.log2(total)

    def partial(p, odd, index):
        bank, h = banks[p], 2 * p + odd
        here = lanes(odd * HEAD_DIM, HEAD_DIM)
        picked = [rows_ref[index, i] for i in range(2 * PLANE)]
        keys = jnp.concatenate([bank[0, r, :, here] for r in picked], axis=0)
        values = jnp.concatenate([bank[1, r, :, here] for r in picked], axis=0)
        biases = [bias_ref[index, i] for i in range(2 * PLANE)]
        return softmax(keys, values, qt[index, h], biases)

    def merge(a, b):
        (oa, la), (ob, lb_) = a, b
        top = jnp.maximum(la, lb_)
        wa, wb = jnp.exp2(la - top), jnp.exp2(lb_ - top)
        total = wa + wb
        return oa * (wa / total) + ob * (wb / total), top + jnp.log2(total)

    def put(s, k, h, part):
        rb[s, k, h] = part[0].astype(jnp.bfloat16)
        for i in range(4):
            lb[s, k, h, i : i + 1, :] = part[1][:, i * 128 : (i + 1) * 128]

    def get(s, k, h):
        lse = jnp.concatenate([lb[s, k, h, i : i + 1, :] for i in range(4)], axis=1)
        return rb[s, k, h].astype(jnp.float32), lse

    def ag_step(p, k):
        for u in side_units(k):
            s, h = u // 2, 2 * p + u % 2
            if k > 1:
                ag(s, k - 1, h).wait_recv()
            ag(s, k, h).start()

    def ag_end(p):
        for u in range(4):
            s, h = u // 2, 2 * p + u % 2
            ag(s, 4 if (u // 2 + u % 2) % 2 == 0 else 3, h).wait_recv()

    def rs_step(p, j):
        units, stride = (4, 1) if j < 3 else (2, 3)

        def unit(i, carry):
            u = i * stride
            s = u // 2
            odd = u % 2
            h = 2 * p + odd
            k = 4 - (s + odd) % 2 - j
            part = partial(p, odd, s * 4 + k)
            if j:
                for copy in back(s, k + 1, h):
                    copy.wait_recv()
                part = merge(get(s, k, h), part)
            put(s, k, h, part)
            for copy in back(s, k, h):
                copy.start()
            return carry

        lax.fori_loop(0, units, unit, 0)

    def home_part(p):
        def one(i, carry):
            h = 2 * p + i
            here = lanes(h * HEAD_DIM, HEAD_DIM)
            part = merge(partial(p, i, 0), softmax(kx[:, here], vx[:, here], qt[0, h], None))
            home[h] = part[0]
            hlse[h] = part[1]
            return carry

        lax.fori_loop(0, 2, one, 0)

    def finish(p):
        def one(i, carry):
            h = 2 * p + i
            here = lanes(h * HEAD_DIM, HEAD_DIM)
            part = (home[h], hlse[h])
            for s in range(2):
                for copy in back(s, 1, h):
                    copy.wait_recv()
                part = merge(part, get(s, 0, h))
            mine[:, here] = jnp.transpose(part[0]).astype(jnp.bfloat16)
            return carry

        lax.fori_loop(0, 2, one, 0)
        for dx in range(1, NX):
            attn_x(p, dx).start()
        attn_own(p).start()

    def bank_start(p):
        for kv in range(2):
            for d in range(2):
                bank_a(p, kv, d).start()
            bank_d(p, kv, 0).start()

    def bank_pass(p):
        for kv in range(2):
            for d in range(2):
                bank_a(p, kv, d).wait_recv()
                bank_b(p, kv, d).start()
                bank_d(p, kv, 1 + d).start()

    def bank_last(p):
        for kv in range(2):
            for d in range(2):
                bank_b(p, kv, d).wait_recv()
                bank_d(p, kv, 3 + d).start()

    def bank_end(p):
        for kv in range(2):
            own_bank(kv, p).wait()
            for t in range(5):
                bank_d(p, kv, t).wait_recv()

    def load_queries(p):
        for dx in range(1, NX):
            x_query(p, dx).wait_recv()
        for h in (2 * p, 2 * p + 1):
            part = qx[:, h * HEAD_DIM : (h + 1) * HEAD_DIM]
            qt[0, h] = jnp.transpose(part.astype(jnp.float32)).astype(jnp.bfloat16)

    for i in range(3):
        own_rows(i).start()
    for p in range(PAIRS):
        for kv in range(2):
            own_bank(kv, p).start()
    w_mine().start()
    barrier = pltpu.get_barrier_semaphore()
    for dev in (dev_x(1), dev_x(2), dev_x(3), sibling, dev_y(1), dev_y(-1), dev_z(1), dev_z(-1)):
        pl.semaphore_signal(barrier, inc=1, device_id=dev, device_id_type=MESH)
    pl.semaphore_wait(barrier, 8)

    for p in range(PAIRS):
        for dx in range(1, NX):
            x_query(p, dx).start()
    bank_start(0)
    for kv in range(2):
        for dx in range(1, NX):
            x_keys(kv, dx).start()
    own_rows(0).wait()
    load_queries(0)
    ag_step(0, 1)
    load_queries(1)
    ag_step(1, 1)
    load_queries(2)
    for dx in range(1, NX):
        w_x(dx).start()
    ag_step(0, 2)
    ag_step(1, 2)
    bank_pass(0)
    bank_start(1)
    ag_step(0, 3)
    ag_step(1, 3)
    bank_last(0)
    ag_step(0, 4)
    ag_step(1, 4)
    ag_step(2, 1)
    bank_end(0)
    ag_end(0)
    rs_step(0, 0)
    ag_step(2, 2)
    bank_pass(1)
    bank_start(2)
    rs_step(0, 1)
    ag_step(2, 3)
    for i in (1, 2):
        own_rows(i).wait()
    for kv in range(2):
        for dx in range(1, NX):
            x_keys(kv, dx).wait_recv()
    home_part(0)
    bank_last(1)
    rs_step(0, 2)
    ag_step(2, 4)
    bank_end(1)
    ag_end(1)
    rs_step(1, 0)
    rs_step(0, 3)
    bank_pass(2)
    ag_end(2)
    home_part(1)
    rs_step(1, 1)
    bank_last(2)
    bank_end(2)
    rs_step(2, 0)
    finish(0)
    rs_step(1, 2)
    rs_step(2, 1)
    home_part(2)
    rs_step(1, 3)
    rs_step(2, 2)
    for dx in range(1, NX):
        w_x(dx).wait_recv()
        w_d(dx).start()
    rs_step(2, 3)
    finish(1)
    finish(2)

    for p in range(PAIRS):
        for dx in range(1, NX):
            x_query(p, dx).wait_send()
            attn_x(p, dx).wait()
        attn_own(p).wait()
        for kv in range(2):
            for d in range(2):
                bank_a(p, kv, d).wait_send()
                bank_b(p, kv, d).wait_send()
            for t in range(5):
                bank_d(p, kv, t).wait_send()
        for k in range(1, 5):
            for u in side_units(k):
                s, h = u // 2, 2 * p + u % 2
                ag(s, k, h).wait_send()
                for copy in back(s, k, h):
                    copy.wait_send()
    for dx in range(1, NX):
        for kv in range(2):
            x_keys(kv, dx).wait_send()
        w_x(dx).wait_send()
        w_d(dx).wait()
    w_mine().wait()


def plan(frame_slot, picks, counts, per_device):
    frame = lax.axis_index("frame")
    y, z, c = frame // (NZ * NC), (frame // NC) % NZ, frame % NC
    longest = picks.shape[1]
    offsets = jnp.array([0, 1, 2, 3, 4, -1, -2, -3, -4], jnp.int32)
    spans = (y * NZ + (z + offsets + NZ) % NZ) * NC + c
    listed = picks[spans]
    number = counts[spans]
    table = jnp.arange(frame_slot.shape[0], dtype=jnp.int32)
    hits = listed[:, :, None] == table[None, None, :]
    bank_rows = jnp.sum(jnp.where(hits, frame_slot[None, None, :], 0), axis=2)
    position = jnp.arange(longest, dtype=jnp.int32)
    owner = bank_rows // per_device
    here = (position[None, :] < number[:, None]) & ((owner // NC) % NZ == z)
    earlier = here[:, None, :] & (position[None, None, :] < position[None, :, None])
    rank = jnp.sum(earlier.astype(jnp.int32), axis=2)
    local = (owner // (NZ * NC) * NC + owner % NC) * per_device + bank_rows % per_device
    slots = jnp.arange(2 * PLANE, dtype=jnp.int32)
    chosen = here[:, None, :] & (rank[:, None, :] == slots[None, :, None])
    rows = jnp.sum(jnp.where(chosen, local[:, None, :], 0), axis=2)
    bias = jnp.where(jnp.any(chosen, axis=2), 0.0, NEG).astype(jnp.float32)
    return rows, bias


def local(span_q, span_k, span_v, bank_k, bank_v, frame_slot, picks, counts, out_weight):
    rows, bias = plan(frame_slot, picks, counts, bank_k.shape[0])
    width = bank_k.shape[2]
    heads = width // HEAD_DIM
    span_rows = span_q.shape[0] * NX
    model = span_q.shape[1]
    bf, dma = jnp.bfloat16, pltpu.SemaphoreType.DMA
    smem = pl.BlockSpec(memory_space=pltpu.SMEM)
    hbm = pl.BlockSpec(memory_space=pl.ANY)
    attn, weight = pl.pallas_call(
        kernel,
        out_shape=(
            jax.ShapeDtypeStruct((span_q.shape[0], model), bf),
            jax.ShapeDtypeStruct((model, out_weight.shape[1]), bf),
        ),
        in_specs=[smem, smem] + [hbm] * 6,
        out_specs=(pl.BlockSpec(memory_space=pltpu.VMEM), hbm),
        scratch_shapes=[
            pltpu.VMEM((span_rows, width), bf),
            pltpu.VMEM((span_rows, width), bf),
            pltpu.VMEM((span_rows, width), bf),
            *[pltpu.VMEM((2, PLANE * bank_k.shape[0], bank_k.shape[1], 256), bf)] * PAIRS,
            pltpu.VMEM((9, heads, HEAD_DIM, span_rows), bf),
            pltpu.VMEM((2, 5, heads, HEAD_DIM, span_rows), bf),
            pltpu.VMEM((2, 5, heads, 4, 128), jnp.float32),
            pltpu.VMEM((heads, HEAD_DIM, span_rows), jnp.float32),
            pltpu.VMEM((heads, 1, span_rows), jnp.float32),
            pltpu.VMEM((span_rows, width), bf),
            dma((PAIRS, NX - 1)), dma((PAIRS, NX - 1)),
            dma((2, NX - 1)), dma((2, NX - 1)),
            dma((3,)), dma((PAIRS, 2)), dma(()),
            dma((NX - 1,)), dma((NX - 1,)), dma((NX - 1,)), dma((NX - 1,)),
            dma((PAIRS, 2, 2)), dma((PAIRS, 2, 2)),
            dma((PAIRS, 2, 2)), dma((PAIRS, 2, 2)),
            dma((PAIRS, 2, 5)), dma((PAIRS, 2, 5)),
            dma((2, 5, heads)), dma((2, 5, heads)),
            dma((2, 5, heads)), dma((2, 5, heads)),
            dma((2, 5, heads)), dma((2, 5, heads)),
            dma((PAIRS, NX - 1)), dma((PAIRS, NX - 1)), dma((PAIRS,)),
        ],
        compiler_params=pltpu.CompilerParams(
            collective_id=0, has_side_effects=True, vmem_limit_bytes=60 * 2**20
        ),
    )(rows, bias, span_q, span_k, span_v, bank_k, bank_v, out_weight)
    return jnp.dot(attn, weight, preferred_element_type=jnp.float32).astype(bf)


def solution(mesh):
    placed = (
        P(("frame", "head"), None),
        P(("frame", "head"), None),
        P(("frame", "head"), None),
        P("frame", None, "head"),
        P("frame", None, "head"),
        P(),
        P(),
        P(),
        P("head", None),
    )
    return jax.shard_map(
        local, mesh=mesh, in_specs=placed, out_specs=P(("frame", "head"), None), check_vma=False
    )
```

```python
import math

import jax
import jax.numpy as jnp
from jax import lax
from jax.experimental import pallas as pl
from jax.experimental.pallas import tpu as pltpu
from jax.sharding import PartitionSpec as P

HEAD_DIM = 128
NX, NY, NZ, NC = 4, 4, 8, 2
PLANE = NY * NC
PAIRS = 3
NEG = -1e30
MESH = pl.DeviceIdType.MESH


def side_units(step):
    return [u for u in range(4) if (4 if (u // 2 + u % 2) % 2 == 0 else 3) >= step]


def kernel(
    rows_ref, bias_ref, q_ref, k_ref, v_ref, bk_ref, bv_ref, w_ref,
    out_ref,
    qx, kx, vx, bank0, bank1, bank2, qt, rb, lb, home, hlse,
    arrived, weight, acc,
    xq_s, xq_r, xk_s, xk_r, own_sem, bo_sem, w_s, w_r, wf_s, wf_r, wd_s, wd_r,
    a_s, a_r, b_s, b_r, d_s, d_r, g_s, g_r, o_s, o_r, l_s, l_r, t_s, t_r, t_own, w_own,
):
    frame = lax.axis_index("frame")
    x = lax.axis_index("head")
    y, z, c = frame // (NZ * NC), (frame // NC) % NZ, frame % NC
    rows = q_ref.shape[0]
    width = qx.shape[1]
    frames = bk_ref.shape[0]
    half = frames // 2
    wrows = w_ref.shape[0]
    whalf = wrows // 2
    mine = qx
    banks = (bank0, bank1, bank2)
    factor = math.log2(math.e) / math.sqrt(HEAD_DIM)

    def dev_y(step):
        return ((((y + step + NY) % NY) * NZ + z) * NC + c, x)

    def dev_z(step):
        return ((y * NZ + (z + step + NZ) % NZ) * NC + c, x)

    def dev_x(step):
        return (frame, (x + step) % NX)

    sibling = ((y * NZ + z) * NC + 1 - c, x)

    def lanes(start, size):
        return pl.ds(pl.multiple_of(start, HEAD_DIM), size)

    def remote(src, dst, s, r, dev):
        return pltpu.make_async_remote_copy(
            src_ref=src, dst_ref=dst, send_sem=s, recv_sem=r, device_id=dev, device_id_type=MESH
        )

    my_rows = pl.ds(pl.multiple_of(x * rows, rows), rows)

    def x_query(p, dx):
        peer = (x + dx) % NX
        return remote(
            q_ref.at[:, lanes(peer * width + p * 256, 256)],
            qx.at[my_rows, pl.ds(p * 256, 256)],
            xq_s.at[p, dx - 1], xq_r.at[p, dx - 1], dev_x(dx),
        )

    def x_keys(kv, dx):
        peer = (x + dx) % NX
        src, dst = ((k_ref, kx), (v_ref, vx))[kv]
        return remote(
            src.at[:, lanes(peer * width, width)], dst.at[my_rows, :],
            xk_s.at[kv, dx - 1], xk_r.at[kv, dx - 1], dev_x(dx),
        )

    def own_rows(i):
        src, dst = ((q_ref, qx), (k_ref, kx), (v_ref, vx))[i]
        return pltpu.make_async_copy(
            src.at[:, lanes(x * width, width)], dst.at[my_rows, :], own_sem.at[i]
        )

    def own_bank(kv, p):
        return pltpu.make_async_copy(
            (bk_ref, bv_ref)[kv].at[:, :, cols(p)], block(kv, y, p), bo_sem.at[p, kv]
        )

    def cols(p):
        return pl.ds(p * 256, 256)

    def block(kv, yy, p):
        return banks[p].at[kv, pl.ds(((yy + NY) % NY * NC + c) * frames, frames)]

    def half_block(kv, yy, which, p):
        start = ((yy + NY) % NY * NC + c) * frames + which * half
        return banks[p].at[kv, pl.ds(start, half)]

    def bank_a(p, kv, d):
        return remote(
            (bk_ref, bv_ref)[kv].at[:, :, cols(p)], block(kv, y, p),
            a_s.at[p, kv, d], a_r.at[p, kv, d], dev_y(1 - 2 * d),
        )

    def bank_b(p, kv, d):
        view = half_block(kv, y - (1 - 2 * d), d, p)
        return remote(view, view, b_s.at[p, kv, d], b_r.at[p, kv, d], dev_y(1 - 2 * d))

    def bank_d(p, kv, t):
        if t == 0:
            src, dst = (bk_ref, bv_ref)[kv].at[:, :, cols(p)], block(kv, y, p)
        elif t <= 2:
            src = dst = block(kv, y - (1 - 2 * (t - 1)), p)
        else:
            src = dst = half_block(kv, y + 2, t - 3, p)
        return remote(src, dst, d_s.at[p, kv, t], d_r.at[p, kv, t], sibling)

    def ag(s, k, h):
        before = 0 if k == 1 else s * 4 + k - 1
        return remote(
            qt.at[before, h], qt.at[s * 4 + k, h], g_s.at[s, k, h], g_r.at[s, k, h], dev_z(2 * s - 1)
        )

    def back(s, k, h):
        return (
            remote(rb.at[s, k, h], rb.at[s, k - 1, h], o_s.at[s, k, h], o_r.at[s, k - 1, h], dev_z(1 - 2 * s)),
            remote(lb.at[s, k, h], lb.at[s, k - 1, h], l_s.at[s, k, h], l_r.at[s, k - 1, h], dev_z(1 - 2 * s)),
        )

    def w_rows(xx, which, part=None):
        size = whalf if part is None else whalf // 2
        start = (xx + NX) % NX * wrows + which * whalf + (0 if part is None else part * size)
        return weight.at[pl.ds(pl.multiple_of(start, whalf // 2), size)]

    def w_x(d):
        return remote(
            w_ref.at[pl.ds(c * whalf, whalf)], w_rows(x, c), w_s.at[d], w_r.at[d], dev_x(1 if d == 0 else NX - 1)
        )

    def w_f(d):
        view = w_rows(x - (1 - 2 * d), c, d)
        return remote(view, view, wf_s.at[d], wf_r.at[d], dev_x(1 if d == 0 else NX - 1))

    def w_d(t):
        view = w_rows(x - (1 - 2 * t), c) if t < 2 else w_rows(x + 2, c)
        return remote(view, view, wd_s.at[t], wd_r.at[t], sibling)

    def attn_x(p, dx):
        peer = (x + dx) % NX
        return remote(
            mine.at[pl.ds(pl.multiple_of(peer * rows, rows), rows), cols(p)],
            arrived.at[:, lanes(x * width + p * 256, 256)],
            t_s.at[p, dx - 1], t_r.at[p, dx - 1], dev_x(dx),
        )

    def attn_own(p):
        return pltpu.make_async_copy(
            mine.at[my_rows, cols(p)], arrived.at[:, lanes(x * width + p * 256, 256)], t_own.at[p]
        )

    def w_mine():
        return pltpu.make_async_copy(w_ref, weight.at[pl.ds(pl.multiple_of(x * wrows, wrows), wrows)], w_own)

    def softmax(keys, values, queries, biases):
        scores = jnp.dot(keys, queries, preferred_element_type=jnp.float32) * factor
        if biases is not None:
            step = scores.shape[0] // len(biases)
            scores = jnp.concatenate(
                [scores[i * step : (i + 1) * step] + b for i, b in enumerate(biases)], axis=0
            )
        top = jnp.max(scores, axis=0, keepdims=True)
        expo = jnp.exp2(scores - top)
        total = jnp.sum(expo, axis=0, keepdims=True)
        numer = lax.dot_general(
            values, expo.astype(jnp.bfloat16), (((0,), (0,)), ((), ())),
            preferred_element_type=jnp.float32,
        )
        return numer / total, top + jnp.log2(total)

    def partial(p, odd, index, away):
        bank, h, where = banks[p], 2 * p + odd, (z + away + NZ) % NZ
        here = lanes(odd * HEAD_DIM, HEAD_DIM)
        picked = [rows_ref[where, i] for i in range(2 * PLANE)]
        keys = jnp.concatenate([bank[0, r, :, here] for r in picked], axis=0)
        values = jnp.concatenate([bank[1, r, :, here] for r in picked], axis=0)
        biases = [bias_ref[where, i] for i in range(2 * PLANE)]
        return softmax(keys, values, qt[index, h], biases)

    def merge(a, b):
        (oa, la), (ob, lb_) = a, b
        top = jnp.maximum(la, lb_)
        wa, wb = jnp.exp2(la - top), jnp.exp2(lb_ - top)
        total = wa + wb
        return oa * (wa / total) + ob * (wb / total), top + jnp.log2(total)

    def put(s, k, h, part):
        rb[s, k, h] = part[0].astype(jnp.bfloat16)
        for i in range(4):
            lb[s, k, h, i : i + 1, :] = part[1][:, i * 128 : (i + 1) * 128]

    def get(s, k, h):
        lse = jnp.concatenate([lb[s, k, h, i : i + 1, :] for i in range(4)], axis=1)
        return rb[s, k, h].astype(jnp.float32), lse

    def ag_step(p, k):
        for u in side_units(k):
            s, h = u // 2, 2 * p + u % 2
            if k > 1:
                ag(s, k - 1, h).wait_recv()
            ag(s, k, h).start()

    def ag_end(p):
        for u in range(4):
            s, h = u // 2, 2 * p + u % 2
            ag(s, 4 if (u // 2 + u % 2) % 2 == 0 else 3, h).wait_recv()

    def rs_step(p, j):
        units, stride = (4, 1) if j < 3 else (2, 3)

        def unit(i, carry):
            u = i * stride
            s = u // 2
            odd = u % 2
            h = 2 * p + odd
            k = 4 - (s + odd) % 2 - j
            part = partial(p, odd, s * 4 + k, k - 2 * s * k)
            if j:
                for copy in back(s, k + 1, h):
                    copy.wait_recv()
                part = merge(get(s, k, h), part)
            put(s, k, h, part)
            for copy in back(s, k, h):
                copy.start()
            return carry

        lax.fori_loop(0, units, unit, 0)

    def home_part(p):
        def one(i, carry):
            h = 2 * p + i
            here = lanes(h * HEAD_DIM, HEAD_DIM)
            part = merge(partial(p, i, 0, 0), softmax(kx[:, here], vx[:, here], qt[0, h], None))
            home[h] = part[0]
            hlse[h] = part[1]
            return carry

        lax.fori_loop(0, 2, one, 0)

    def finish(p):
        def one(i, carry):
            h = 2 * p + i
            here = lanes(h * HEAD_DIM, HEAD_DIM)
            part = (home[h], hlse[h])
            for s in range(2):
                for copy in back(s, 1, h):
                    copy.wait_recv()
                part = merge(part, get(s, 0, h))
            mine[:, here] = jnp.transpose(part[0]).astype(jnp.bfloat16)
            return carry

        lax.fori_loop(0, 2, one, 0)
        for dx in range(1, NX):
            attn_x(p, dx).start()
        attn_own(p).start()

    def w_ready():
        w_mine().wait()
        for t in range(3):
            w_d(t).wait_recv()

    def w_pass():
        for d in range(2):
            w_x(d).wait_recv()
            w_f(d).start()
            w_d(d).start()

    def w_last():
        for d in range(2):
            w_f(d).wait_recv()
        w_d(2).start()

    def project(p):
        for dx in range(1, NX):
            attn_x(p, dx).wait_recv()
        attn_own(p).wait()

        def columns(i, carry):
            here = pl.ds(pl.multiple_of(i * 512, 512), 512)
            part = acc[:, here] if p else 0.0
            for xx in range(NX):
                deep = pl.ds(xx * width + p * 256, 256)
                part = part + jnp.dot(arrived[:, deep], weight[deep, here], preferred_element_type=jnp.float32)
            if p == PAIRS - 1:
                out_ref[:, here] = part.astype(jnp.bfloat16)
            else:
                acc[:, here] = part
            return carry

        lax.fori_loop(0, out_ref.shape[1] // 512, columns, 0)

    def bank_start(p):
        for kv in range(2):
            for d in range(2):
                bank_a(p, kv, d).start()
            bank_d(p, kv, 0).start()

    def bank_pass(p):
        for kv in range(2):
            for d in range(2):
                bank_a(p, kv, d).wait_recv()
                bank_b(p, kv, d).start()
                bank_d(p, kv, 1 + d).start()

    def bank_last(p):
        for kv in range(2):
            for d in range(2):
                bank_b(p, kv, d).wait_recv()
                bank_d(p, kv, 3 + d).start()

    def bank_end(p):
        for kv in range(2):
            own_bank(kv, p).wait()
            for t in range(5):
                bank_d(p, kv, t).wait_recv()

    def load_queries(p):
        for dx in range(1, NX):
            x_query(p, dx).wait_recv()
        for h in (2 * p, 2 * p + 1):
            part = qx[:, h * HEAD_DIM : (h + 1) * HEAD_DIM]
            qt[0, h] = jnp.transpose(part.astype(jnp.float32)).astype(jnp.bfloat16)

    for i in range(3):
        own_rows(i).start()
    for p in range(PAIRS):
        for kv in range(2):
            own_bank(kv, p).start()
    barrier = pltpu.get_barrier_semaphore()
    for dev in (dev_x(1), dev_x(2), dev_x(3), sibling, dev_y(1), dev_y(-1), dev_z(1), dev_z(-1)):
        pl.semaphore_signal(barrier, inc=1, device_id=dev, device_id_type=MESH)
    pl.semaphore_wait(barrier, 8)

    for p in range(PAIRS):
        for dx in range(1, NX):
            x_query(p, dx).start()
    bank_start(0)
    own_rows(0).wait()
    load_queries(0)
    ag_step(0, 1)
    load_queries(1)
    ag_step(1, 1)
    load_queries(2)
    for kv in range(2):
        for dx in range(1, NX):
            x_keys(kv, dx).start()
    w_mine().start()
    for d in range(2):
        w_x(d).start()
    ag_step(0, 2)
    ag_step(1, 2)
    bank_pass(0)
    bank_start(1)
    ag_step(0, 3)
    ag_step(1, 3)
    bank_last(0)
    ag_step(0, 4)
    ag_step(1, 4)
    ag_step(2, 1)
    bank_end(0)
    ag_end(0)
    rs_step(0, 0)
    ag_step(2, 2)
    bank_pass(1)
    bank_start(2)
    rs_step(0, 1)
    ag_step(2, 3)
    for i in (1, 2):
        own_rows(i).wait()
    for kv in range(2):
        for dx in range(1, NX):
            x_keys(kv, dx).wait_recv()
    home_part(0)
    bank_last(1)
    rs_step(0, 2)
    ag_step(2, 4)
    bank_end(1)
    ag_end(1)
    rs_step(1, 0)
    rs_step(0, 3)
    bank_pass(2)
    ag_end(2)
    home_part(1)
    rs_step(1, 1)
    w_pass()
    bank_last(2)
    bank_end(2)
    rs_step(2, 0)
    finish(0)
    rs_step(1, 2)
    rs_step(2, 1)
    home_part(2)
    rs_step(1, 3)
    w_last()
    rs_step(2, 2)
    finish(1)
    w_ready()
    rs_step(2, 3)
    project(0)
    project(1)
    finish(2)
    project(2)

    for p in range(PAIRS):
        for dx in range(1, NX):
            x_query(p, dx).wait_send()
            attn_x(p, dx).wait_send()
        for kv in range(2):
            for d in range(2):
                bank_a(p, kv, d).wait_send()
                bank_b(p, kv, d).wait_send()
            for t in range(5):
                bank_d(p, kv, t).wait_send()
        for k in range(1, 5):
            for u in side_units(k):
                s, h = u // 2, 2 * p + u % 2
                ag(s, k, h).wait_send()
                for copy in back(s, k, h):
                    copy.wait_send()
    for dx in range(1, NX):
        for kv in range(2):
            x_keys(kv, dx).wait_send()
    for d in range(2):
        w_x(d).wait_send()
        w_f(d).wait_send()
    for t in range(3):
        w_d(t).wait_send()


def plan(frame_slot, picks, counts, per_device):
    frame = lax.axis_index("frame")
    y, z, c = frame // (NZ * NC), (frame // NC) % NZ, frame % NC
    longest = picks.shape[1]
    listed = lax.dynamic_slice(picks.reshape(NY, NZ, NC, longest), (y, 0, c, 0), (1, NZ, 1, longest))
    listed = listed.reshape(NZ, longest)
    number = lax.dynamic_slice(counts.reshape(NY, NZ, NC), (y, 0, c), (1, NZ, 1)).reshape(NZ)
    table = jnp.arange(frame_slot.shape[0], dtype=jnp.int32)
    hits = listed[:, :, None] == table[None, None, :]
    bank_rows = jnp.sum(jnp.where(hits, frame_slot[None, None, :], 0), axis=2)
    position = jnp.arange(longest, dtype=jnp.int32)
    owner = bank_rows // per_device
    here = (position[None, :] < number[:, None]) & ((owner // NC) % NZ == z)
    earlier = here[:, None, :] & (position[None, None, :] < position[None, :, None])
    rank = jnp.sum(earlier.astype(jnp.int32), axis=2)
    local = (owner // (NZ * NC) * NC + owner % NC) * per_device + bank_rows % per_device
    slots = jnp.arange(2 * PLANE, dtype=jnp.int32)
    chosen = here[:, None, :] & (rank[:, None, :] == slots[None, :, None])
    rows = jnp.sum(jnp.where(chosen, local[:, None, :], 0), axis=2)
    bias = jnp.where(jnp.any(chosen, axis=2), 0.0, NEG).astype(jnp.float32)
    return rows, bias


def local(span_q, span_k, span_v, bank_k, bank_v, frame_slot, picks, counts, out_weight):
    rows, bias = plan(frame_slot, picks, counts, bank_k.shape[0])
    width = bank_k.shape[2]
    heads = width // HEAD_DIM
    span_rows = span_q.shape[0] * NX
    model = span_q.shape[1]
    bf, dma = jnp.bfloat16, pltpu.SemaphoreType.DMA
    smem = pl.BlockSpec(memory_space=pltpu.SMEM)
    hbm = pl.BlockSpec(memory_space=pl.ANY)
    return pl.pallas_call(
        kernel,
        out_shape=jax.ShapeDtypeStruct((span_q.shape[0], out_weight.shape[1]), bf),
        in_specs=[smem, smem] + [hbm] * 6,
        out_specs=pl.BlockSpec(memory_space=pltpu.VMEM),
        scratch_shapes=[
            pltpu.VMEM((span_rows, width), bf),
            pltpu.VMEM((span_rows, width), bf),
            pltpu.VMEM((span_rows, width), bf),
            *[pltpu.VMEM((2, PLANE * bank_k.shape[0], bank_k.shape[1], 256), bf)] * PAIRS,
            pltpu.VMEM((9, heads, HEAD_DIM, span_rows), bf),
            pltpu.VMEM((2, 5, heads, HEAD_DIM, span_rows), bf),
            pltpu.VMEM((2, 5, heads, 4, 128), jnp.float32),
            pltpu.VMEM((heads, HEAD_DIM, span_rows), jnp.float32),
            pltpu.VMEM((heads, 1, span_rows), jnp.float32),
            pltpu.VMEM((span_q.shape[0], model), bf),
            pltpu.VMEM((model, out_weight.shape[1]), bf),
            pltpu.VMEM((span_q.shape[0], out_weight.shape[1]), jnp.float32),
            dma((PAIRS, NX - 1)), dma((PAIRS, NX - 1)),
            dma((2, NX - 1)), dma((2, NX - 1)),
            dma((3,)), dma((PAIRS, 2)),
            dma((2,)), dma((2,)), dma((2,)), dma((2,)), dma((3,)), dma((3,)),
            dma((PAIRS, 2, 2)), dma((PAIRS, 2, 2)),
            dma((PAIRS, 2, 2)), dma((PAIRS, 2, 2)),
            dma((PAIRS, 2, 5)), dma((PAIRS, 2, 5)),
            dma((2, 5, heads)), dma((2, 5, heads)),
            dma((2, 5, heads)), dma((2, 5, heads)),
            dma((2, 5, heads)), dma((2, 5, heads)),
            dma((PAIRS, NX - 1)), dma((PAIRS, NX - 1)), dma((PAIRS,)), dma(()),
        ],
        compiler_params=pltpu.CompilerParams(
            collective_id=0, has_side_effects=True, vmem_limit_bytes=63 * 2**20
        ),
    )(rows, bias, span_q, span_k, span_v, bank_k, bank_v, out_weight)


def solution(mesh):
    placed = (
        P(("frame", "head"), None),
        P(("frame", "head"), None),
        P(("frame", "head"), None),
        P("frame", None, "head"),
        P("frame", None, "head"),
        P(),
        P(),
        P(),
        P("head", None),
    )
    return jax.shard_map(
        local, mesh=mesh, in_specs=placed, out_specs=P(("frame", "head"), None), check_vma=False
    )
```

```python
import math

import jax
import jax.numpy as jnp
from jax import lax
from jax.experimental import pallas as pl
from jax.experimental.pallas import tpu as pltpu
from jax.sharding import PartitionSpec as P

HEAD_DIM = 128
NX, NY, NZ, NC = 4, 4, 8, 2
PLANE = NY * NC
PAIRS = 3
NEG = -1e30
MESH = pl.DeviceIdType.MESH


def side_units(step):
    return [u for u in range(4) if (4 if (u // 2 + u % 2) % 2 == 0 else 3) >= step]


def kernel(
    picks_ref, counts_ref, slot_ref, q_ref, k_ref, v_ref, bk_ref, bv_ref, w_ref,
    out_ref,
    qx, kx, vx, bank0, bank1, bank2, qt, rb, lb, home, hlse,
    arrived, weight, acc, table_v, table,
    xq_s, xq_r, xk_s, xk_r, own_sem, bo_sem, w_s, w_r, wf_s, wf_r, wd_s, wd_r,
    a_s, a_r, b_s, b_r, d_s, d_r, g_s, g_r, o_s, o_r, l_s, l_r, t_s, t_r, t_own, w_own, table_sem,
):
    frame = lax.axis_index("frame")
    x = lax.axis_index("head")
    y, z, c = frame // (NZ * NC), (frame // NC) % NZ, frame % NC
    rows = q_ref.shape[0]
    width = qx.shape[1]
    frames = bk_ref.shape[0]
    half = frames // 2
    wrows = w_ref.shape[0]
    whalf = wrows // 2
    mine = qx
    banks = (bank0, bank1, bank2)
    factor = math.log2(math.e) / math.sqrt(HEAD_DIM)

    def dev_y(step):
        return ((((y + step + NY) % NY) * NZ + z) * NC + c, x)

    def dev_z(step):
        return ((y * NZ + (z + step + NZ) % NZ) * NC + c, x)

    def dev_x(step):
        return (frame, (x + step) % NX)

    sibling = ((y * NZ + z) * NC + 1 - c, x)

    def lanes(start, size):
        return pl.ds(pl.multiple_of(start, HEAD_DIM), size)

    def remote(src, dst, s, r, dev):
        return pltpu.make_async_remote_copy(
            src_ref=src, dst_ref=dst, send_sem=s, recv_sem=r, device_id=dev, device_id_type=MESH
        )

    my_rows = pl.ds(pl.multiple_of(x * rows, rows), rows)

    def x_query(p, dx):
        peer = (x + dx) % NX
        return remote(
            q_ref.at[:, lanes(peer * width + p * 256, 256)],
            qx.at[my_rows, pl.ds(p * 256, 256)],
            xq_s.at[p, dx - 1], xq_r.at[p, dx - 1], dev_x(dx),
        )

    def x_keys(kv, dx):
        peer = (x + dx) % NX
        src, dst = ((k_ref, kx), (v_ref, vx))[kv]
        return remote(
            src.at[:, lanes(peer * width, width)], dst.at[my_rows, :],
            xk_s.at[kv, dx - 1], xk_r.at[kv, dx - 1], dev_x(dx),
        )

    def own_rows(i):
        src, dst = ((q_ref, qx), (k_ref, kx), (v_ref, vx))[i]
        return pltpu.make_async_copy(
            src.at[:, lanes(x * width, width)], dst.at[my_rows, :], own_sem.at[i]
        )

    def own_bank(kv, p):
        return pltpu.make_async_copy(
            (bk_ref, bv_ref)[kv].at[:, :, cols(p)], block(kv, y, p), bo_sem.at[p, kv]
        )

    def cols(p):
        return pl.ds(p * 256, 256)

    def block(kv, yy, p):
        return banks[p].at[kv, pl.ds(((yy + NY) % NY * NC + c) * frames, frames)]

    def half_block(kv, yy, which, p):
        start = ((yy + NY) % NY * NC + c) * frames + which * half
        return banks[p].at[kv, pl.ds(start, half)]

    def bank_a(p, kv, d):
        return remote(
            (bk_ref, bv_ref)[kv].at[:, :, cols(p)], block(kv, y, p),
            a_s.at[p, kv, d], a_r.at[p, kv, d], dev_y(1 - 2 * d),
        )

    def bank_b(p, kv, d):
        view = half_block(kv, y - (1 - 2 * d), d, p)
        return remote(view, view, b_s.at[p, kv, d], b_r.at[p, kv, d], dev_y(1 - 2 * d))

    def bank_d(p, kv, t):
        if t == 0:
            src, dst = (bk_ref, bv_ref)[kv].at[:, :, cols(p)], block(kv, y, p)
        elif t <= 2:
            src = dst = block(kv, y - (1 - 2 * (t - 1)), p)
        else:
            src = dst = half_block(kv, y + 2, t - 3, p)
        return remote(src, dst, d_s.at[p, kv, t], d_r.at[p, kv, t], sibling)

    def ag(s, k, h):
        before = 0 if k == 1 else s * 4 + k - 1
        return remote(
            qt.at[before, h], qt.at[s * 4 + k, h], g_s.at[s, k, h], g_r.at[s, k, h], dev_z(2 * s - 1)
        )

    def back(s, k, h):
        return (
            remote(rb.at[s, k, h], rb.at[s, k - 1, h], o_s.at[s, k, h], o_r.at[s, k - 1, h], dev_z(1 - 2 * s)),
            remote(lb.at[s, k, h], lb.at[s, k - 1, h], l_s.at[s, k, h], l_r.at[s, k - 1, h], dev_z(1 - 2 * s)),
        )

    def w_rows(xx, which, part=None):
        size = whalf if part is None else whalf // 2
        start = (xx + NX) % NX * wrows + which * whalf + (0 if part is None else part * size)
        return weight.at[pl.ds(pl.multiple_of(start, whalf // 2), size)]

    def w_x(d):
        return remote(
            w_ref.at[pl.ds(c * whalf, whalf)], w_rows(x, c), w_s.at[d], w_r.at[d], dev_x(1 if d == 0 else NX - 1)
        )

    def w_f(d):
        view = w_rows(x - (1 - 2 * d), c, d)
        return remote(view, view, wf_s.at[d], wf_r.at[d], dev_x(1 if d == 0 else NX - 1))

    def w_d(t):
        view = w_rows(x - (1 - 2 * t), c) if t < 2 else w_rows(x + 2, c)
        return remote(view, view, wd_s.at[t], wd_r.at[t], sibling)

    def attn_x(p, dx):
        peer = (x + dx) % NX
        return remote(
            mine.at[pl.ds(pl.multiple_of(peer * rows, rows), rows), cols(p)],
            arrived.at[:, lanes(x * width + p * 256, 256)],
            t_s.at[p, dx - 1], t_r.at[p, dx - 1], dev_x(dx),
        )

    def attn_own(p):
        return pltpu.make_async_copy(
            mine.at[my_rows, cols(p)], arrived.at[:, lanes(x * width + p * 256, 256)], t_own.at[p]
        )

    def w_mine():
        return pltpu.make_async_copy(w_ref, weight.at[pl.ds(pl.multiple_of(x * wrows, wrows), wrows)], w_own)

    def softmax(keys, values, queries, biases):
        scores = jnp.dot(keys, queries, preferred_element_type=jnp.float32) * factor
        if biases is not None:
            step = scores.shape[0] // len(biases)
            scores = jnp.concatenate(
                [scores[i * step : (i + 1) * step] + b for i, b in enumerate(biases)], axis=0
            )
        top = jnp.max(scores, axis=0, keepdims=True)
        expo = jnp.exp2(scores - top)
        total = jnp.sum(expo, axis=0, keepdims=True)
        numer = lax.dot_general(
            values, expo.astype(jnp.bfloat16), (((0,), (0,)), ((), ())),
            preferred_element_type=jnp.float32,
        )
        return numer / total, top + jnp.log2(total)

    def partial(p, odd, index, away):
        bank, h, where = banks[p], 2 * p + odd, (z + away + NZ) % NZ
        here = lanes(odd * HEAD_DIM, HEAD_DIM)
        listed = [table[where, i] for i in range(2 * PLANE)]
        picked = [jnp.maximum(r, 0) for r in listed]
        keys = jnp.concatenate([bank[0, r, :, here] for r in picked], axis=0)
        values = jnp.concatenate([bank[1, r, :, here] for r in picked], axis=0)
        biases = [jnp.where(r < 0, NEG, 0.0) for r in listed]
        return softmax(keys, values, qt[index, h], biases)

    def merge(a, b):
        (oa, la), (ob, lb_) = a, b
        top = jnp.maximum(la, lb_)
        wa, wb = jnp.exp2(la - top), jnp.exp2(lb_ - top)
        total = wa + wb
        return oa * (wa / total) + ob * (wb / total), top + jnp.log2(total)

    def put(s, k, h, part):
        rb[s, k, h] = part[0].astype(jnp.bfloat16)
        for i in range(4):
            lb[s, k, h, i : i + 1, :] = part[1][:, i * 128 : (i + 1) * 128]

    def get(s, k, h):
        lse = jnp.concatenate([lb[s, k, h, i : i + 1, :] for i in range(4)], axis=1)
        return rb[s, k, h].astype(jnp.float32), lse

    def plan():
        first = y * NZ * NC + c
        listed = picks_ref[pl.ds(first, NZ, stride=NC), :]
        span = lax.broadcasted_iota(jnp.int32, listed.shape, 0)
        position = lax.broadcasted_iota(jnp.int32, listed.shape, 1)
        number = jnp.zeros(listed.shape, jnp.int32)
        for i in range(NZ):
            number = jnp.where(span == i, counts_ref[first + i * NC], number)

        def look(i, found):
            for j in range(8):
                t = i * 8 + j
                found = jnp.where(listed == t, slot_ref[t], found)
            return found

        found = lax.fori_loop(0, slot_ref.shape[0] // 8, look, jnp.zeros(listed.shape, jnp.int32))
        magic = -(-65536 // frames)
        owner = (found * magic) >> 16
        here = (position < number) & (((owner >> 1) & (NZ - 1)) == z)
        holder = ((owner >> 4) << 1) + (owner & 1)
        place = holder * frames + found - owner * frames
        lane = lax.broadcasted_iota(jnp.int32, table_v.shape, 1)
        out = jnp.full(table_v.shape, -1, jnp.int32)
        for m in range(PLANE):
            mine_here = here & (holder == m)
            high = jnp.max(jnp.where(mine_here, place, -1), axis=1, keepdims=True)
            low = jnp.min(jnp.where(mine_here, place, 1 << 20), axis=1, keepdims=True)
            out = jnp.where(lane == 2 * m, high, out)
            out = jnp.where(lane == 2 * m + 1, jnp.where(low < high, low, -1), out)
        table_v[...] = out
        copy = pltpu.make_async_copy(table_v, table, table_sem)
        copy.start()
        copy.wait()

    def ag_step(p, k):
        for u in side_units(k):
            s, h = u // 2, 2 * p + u % 2
            if k > 1:
                ag(s, k - 1, h).wait_recv()
            ag(s, k, h).start()

    def ag_end(p):
        for u in range(4):
            s, h = u // 2, 2 * p + u % 2
            ag(s, 4 if (u // 2 + u % 2) % 2 == 0 else 3, h).wait_recv()

    def rs_step(p, j):
        units, stride = (4, 1) if j < 3 else (2, 3)

        def unit(i, carry):
            u = i * stride
            s = u // 2
            odd = u % 2
            h = 2 * p + odd
            k = 4 - (s + odd) % 2 - j
            part = partial(p, odd, s * 4 + k, k - 2 * s * k)
            if j:
                for copy in back(s, k + 1, h):
                    copy.wait_recv()
                part = merge(get(s, k, h), part)
            put(s, k, h, part)
            for copy in back(s, k, h):
                copy.start()
            return carry

        lax.fori_loop(0, units, unit, 0)

    def home_part(p):
        def one(i, carry):
            h = 2 * p + i
            here = lanes(h * HEAD_DIM, HEAD_DIM)
            part = merge(partial(p, i, 0, 0), softmax(kx[:, here], vx[:, here], qt[0, h], None))
            home[h] = part[0]
            hlse[h] = part[1]
            return carry

        lax.fori_loop(0, 2, one, 0)

    def finish(p):
        def one(i, carry):
            h = 2 * p + i
            here = lanes(h * HEAD_DIM, HEAD_DIM)
            part = (home[h], hlse[h])
            for s in range(2):
                for copy in back(s, 1, h):
                    copy.wait_recv()
                part = merge(part, get(s, 0, h))
            mine[:, here] = jnp.transpose(part[0]).astype(jnp.bfloat16)
            return carry

        lax.fori_loop(0, 2, one, 0)
        for dx in range(1, NX):
            attn_x(p, dx).start()
        attn_own(p).start()

    def w_ready():
        w_mine().wait()
        for t in range(3):
            w_d(t).wait_recv()

    def w_pass():
        for d in range(2):
            w_x(d).wait_recv()
            w_f(d).start()
            w_d(d).start()

    def w_last():
        for d in range(2):
            w_f(d).wait_recv()
        w_d(2).start()

    def project(p):
        for dx in range(1, NX):
            attn_x(p, dx).wait_recv()
        attn_own(p).wait()

        def columns(i, carry):
            here = pl.ds(pl.multiple_of(i * 512, 512), 512)
            part = acc[:, here] if p else 0.0
            for xx in range(NX):
                deep = pl.ds(xx * width + p * 256, 256)
                part = part + jnp.dot(arrived[:, deep], weight[deep, here], preferred_element_type=jnp.float32)
            if p == PAIRS - 1:
                out_ref[:, here] = part.astype(jnp.bfloat16)
            else:
                acc[:, here] = part
            return carry

        lax.fori_loop(0, out_ref.shape[1] // 512, columns, 0)

    def bank_start(p):
        for kv in range(2):
            for d in range(2):
                bank_a(p, kv, d).start()
            bank_d(p, kv, 0).start()

    def bank_pass(p):
        for kv in range(2):
            for d in range(2):
                bank_a(p, kv, d).wait_recv()
                bank_b(p, kv, d).start()
                bank_d(p, kv, 1 + d).start()

    def bank_last(p):
        for kv in range(2):
            for d in range(2):
                bank_b(p, kv, d).wait_recv()
                bank_d(p, kv, 3 + d).start()

    def bank_end(p):
        for kv in range(2):
            own_bank(kv, p).wait()
            for t in range(5):
                bank_d(p, kv, t).wait_recv()

    def load_queries(p):
        for dx in range(1, NX):
            x_query(p, dx).wait_recv()
        for h in (2 * p, 2 * p + 1):
            part = qx[:, h * HEAD_DIM : (h + 1) * HEAD_DIM]
            qt[0, h] = jnp.transpose(part.astype(jnp.float32)).astype(jnp.bfloat16)

    for i in range(3):
        own_rows(i).start()
    for p in range(PAIRS):
        for kv in range(2):
            own_bank(kv, p).start()
    barrier = pltpu.get_barrier_semaphore()
    for dev in (dev_x(1), dev_x(2), dev_x(3), sibling, dev_y(1), dev_y(-1), dev_z(1), dev_z(-1)):
        pl.semaphore_signal(barrier, inc=1, device_id=dev, device_id_type=MESH)
    pl.semaphore_wait(barrier, 8)

    for p in range(PAIRS):
        for dx in range(1, NX):
            x_query(p, dx).start()
    bank_start(0)
    own_rows(0).wait()
    load_queries(0)
    ag_step(0, 1)
    load_queries(1)
    ag_step(1, 1)
    load_queries(2)
    for kv in range(2):
        for dx in range(1, NX):
            x_keys(kv, dx).start()
    w_mine().start()
    for d in range(2):
        w_x(d).start()
    plan()
    ag_step(0, 2)
    ag_step(1, 2)
    bank_pass(0)
    bank_start(1)
    ag_step(0, 3)
    ag_step(1, 3)
    bank_last(0)
    ag_step(0, 4)
    ag_step(1, 4)
    ag_step(2, 1)
    bank_end(0)
    ag_end(0)
    rs_step(0, 0)
    ag_step(2, 2)
    bank_pass(1)
    bank_start(2)
    rs_step(0, 1)
    ag_step(2, 3)
    for i in (1, 2):
        own_rows(i).wait()
    for kv in range(2):
        for dx in range(1, NX):
            x_keys(kv, dx).wait_recv()
    home_part(0)
    bank_last(1)
    rs_step(0, 2)
    ag_step(2, 4)
    bank_end(1)
    ag_end(1)
    rs_step(1, 0)
    rs_step(0, 3)
    bank_pass(2)
    ag_end(2)
    home_part(1)
    rs_step(1, 1)
    w_pass()
    bank_last(2)
    bank_end(2)
    rs_step(2, 0)
    finish(0)
    rs_step(1, 2)
    rs_step(2, 1)
    home_part(2)
    rs_step(1, 3)
    w_last()
    rs_step(2, 2)
    finish(1)
    rs_step(2, 3)
    finish(2)
    w_ready()
    project(0)
    project(1)
    project(2)

    for p in range(PAIRS):
        for dx in range(1, NX):
            x_query(p, dx).wait_send()
            attn_x(p, dx).wait_send()
        for kv in range(2):
            for d in range(2):
                bank_a(p, kv, d).wait_send()
                bank_b(p, kv, d).wait_send()
            for t in range(5):
                bank_d(p, kv, t).wait_send()
        for k in range(1, 5):
            for u in side_units(k):
                s, h = u // 2, 2 * p + u % 2
                ag(s, k, h).wait_send()
                for copy in back(s, k, h):
                    copy.wait_send()
    for dx in range(1, NX):
        for kv in range(2):
            x_keys(kv, dx).wait_send()
    for d in range(2):
        w_x(d).wait_send()
        w_f(d).wait_send()
    for t in range(3):
        w_d(t).wait_send()


def local(span_q, span_k, span_v, bank_k, bank_v, frame_slot, picks, counts, out_weight):
    width = bank_k.shape[2]
    heads = width // HEAD_DIM
    span_rows = span_q.shape[0] * NX
    model = span_q.shape[1]
    bf, dma = jnp.bfloat16, pltpu.SemaphoreType.DMA
    smem = pl.BlockSpec(memory_space=pltpu.SMEM)
    hbm = pl.BlockSpec(memory_space=pl.ANY)
    return pl.pallas_call(
        kernel,
        out_shape=jax.ShapeDtypeStruct((span_q.shape[0], out_weight.shape[1]), bf),
        in_specs=[pl.BlockSpec(memory_space=pltpu.VMEM), smem, smem] + [hbm] * 6,
        out_specs=pl.BlockSpec(memory_space=pltpu.VMEM),
        scratch_shapes=[
            pltpu.VMEM((span_rows, width), bf),
            pltpu.VMEM((span_rows, width), bf),
            pltpu.VMEM((span_rows, width), bf),
            *[pltpu.VMEM((2, PLANE * bank_k.shape[0], bank_k.shape[1], 256), bf)] * PAIRS,
            pltpu.VMEM((9, heads, HEAD_DIM, span_rows), bf),
            pltpu.VMEM((2, 5, heads, HEAD_DIM, span_rows), bf),
            pltpu.VMEM((2, 5, heads, 4, 128), jnp.float32),
            pltpu.VMEM((heads, HEAD_DIM, span_rows), jnp.float32),
            pltpu.VMEM((heads, 1, span_rows), jnp.float32),
            pltpu.VMEM((span_q.shape[0], model), bf),
            pltpu.VMEM((model, out_weight.shape[1]), bf),
            pltpu.VMEM((span_q.shape[0], out_weight.shape[1]), jnp.float32),
            pltpu.VMEM((NZ, 128), jnp.int32),
            pltpu.SMEM((NZ, 128), jnp.int32),
            dma((PAIRS, NX - 1)), dma((PAIRS, NX - 1)),
            dma((2, NX - 1)), dma((2, NX - 1)),
            dma((3,)), dma((PAIRS, 2)),
            dma((2,)), dma((2,)), dma((2,)), dma((2,)), dma((3,)), dma((3,)),
            dma((PAIRS, 2, 2)), dma((PAIRS, 2, 2)),
            dma((PAIRS, 2, 2)), dma((PAIRS, 2, 2)),
            dma((PAIRS, 2, 5)), dma((PAIRS, 2, 5)),
            dma((2, 5, heads)), dma((2, 5, heads)),
            dma((2, 5, heads)), dma((2, 5, heads)),
            dma((2, 5, heads)), dma((2, 5, heads)),
            dma((PAIRS, NX - 1)), dma((PAIRS, NX - 1)), dma((PAIRS,)), dma(()), dma(()),
        ],
        compiler_params=pltpu.CompilerParams(
            collective_id=0, has_side_effects=True, vmem_limit_bytes=63 * 2**20
        ),
    )(picks, counts, frame_slot, span_q, span_k, span_v, bank_k, bank_v, out_weight)


def solution(mesh):
    placed = (
        P(("frame", "head"), None),
        P(("frame", "head"), None),
        P(("frame", "head"), None),
        P("frame", None, "head"),
        P("frame", None, "head"),
        P(),
        P(),
        P(),
        P("head", None),
    )
    return jax.shard_map(
        local, mesh=mesh, in_specs=placed, out_specs=P(("frame", "head"), None), check_vma=False
    )
```

```python
import math

import jax
import jax.numpy as jnp
from jax import lax
from jax.experimental import pallas as pl
from jax.experimental.pallas import tpu as pltpu
from jax.sharding import PartitionSpec as P

HEAD_DIM = 128
NX, NY, NZ, NC = 4, 4, 8, 2
PLANE = NY * NC
PAIRS = 3
NEG = -1e30
MESH = pl.DeviceIdType.MESH


def side_units(step):
    return [u for u in range(4) if (4 if (u // 2 + u % 2) % 2 == 0 else 3) >= step]


def kernel(
    picks_ref, counts_ref, slot_ref, q_ref, k_ref, v_ref, bk_ref, bv_ref, w_ref,
    out_ref,
    qx, kx, vx, bank0, bank1, bank2, qt, rb, lb, home, hlse,
    arrived, weight, acc, table_v, table,
    xq_s, xq_r, xk_s, xk_r, own_sem, bo_sem, w_s, w_r, wf_s, wf_r, wd_s, wd_r,
    a_s, a_r, b_s, b_r, d_s, d_r, g_s, g_r, o_s, o_r, l_s, l_r, t_s, t_r, t_own, w_own, table_sem,
):
    frame = lax.axis_index("frame")
    x = lax.axis_index("head")
    y, z, c = frame // (NZ * NC), (frame // NC) % NZ, frame % NC
    rows = q_ref.shape[0]
    width = qx.shape[1]
    frames = bk_ref.shape[0]
    half = frames // 2
    wrows = w_ref.shape[0]
    whalf = wrows // 2
    mine = qx
    banks = (bank0, bank1, bank2)
    factor = math.log2(math.e) / math.sqrt(HEAD_DIM)

    def dev_y(step):
        return ((((y + step + NY) % NY) * NZ + z) * NC + c, x)

    def dev_z(step):
        return ((y * NZ + (z + step + NZ) % NZ) * NC + c, x)

    def dev_x(step):
        return (frame, (x + step) % NX)

    sibling = ((y * NZ + z) * NC + 1 - c, x)

    def lanes(start, size):
        return pl.ds(pl.multiple_of(start, HEAD_DIM), size)

    def remote(src, dst, s, r, dev):
        return pltpu.make_async_remote_copy(
            src_ref=src, dst_ref=dst, send_sem=s, recv_sem=r, device_id=dev, device_id_type=MESH
        )

    my_rows = pl.ds(pl.multiple_of(x * rows, rows), rows)

    def x_query(p, dx):
        peer = (x + dx) % NX
        return remote(
            q_ref.at[:, lanes(peer * width + p * 256, 256)],
            qx.at[my_rows, pl.ds(p * 256, 256)],
            xq_s.at[p, dx - 1], xq_r.at[p, dx - 1], dev_x(dx),
        )

    def x_keys(kv, dx):
        peer = (x + dx) % NX
        src, dst = ((k_ref, kx), (v_ref, vx))[kv]
        return remote(
            src.at[:, lanes(peer * width, width)], dst.at[my_rows, :],
            xk_s.at[kv, dx - 1], xk_r.at[kv, dx - 1], dev_x(dx),
        )

    def own_rows(i):
        src, dst = ((q_ref, qx), (k_ref, kx), (v_ref, vx))[i]
        return pltpu.make_async_copy(
            src.at[:, lanes(x * width, width)], dst.at[my_rows, :], own_sem.at[i]
        )

    def own_bank(kv, p):
        return pltpu.make_async_copy(
            (bk_ref, bv_ref)[kv].at[:, :, cols(p)], block(kv, y, p), bo_sem.at[p, kv]
        )

    def cols(p):
        return pl.ds(p * 256, 256)

    def block(kv, yy, p):
        return banks[p].at[kv, pl.ds(((yy + NY) % NY * NC + c) * frames, frames)]

    def half_block(kv, yy, which, p):
        start = ((yy + NY) % NY * NC + c) * frames + which * half
        return banks[p].at[kv, pl.ds(start, half)]

    def bank_a(p, kv, d):
        return remote(
            (bk_ref, bv_ref)[kv].at[:, :, cols(p)], block(kv, y, p),
            a_s.at[p, kv, d], a_r.at[p, kv, d], dev_y(1 - 2 * d),
        )

    def bank_b(p, kv, d):
        view = half_block(kv, y - (1 - 2 * d), d, p)
        return remote(view, view, b_s.at[p, kv, d], b_r.at[p, kv, d], dev_y(1 - 2 * d))

    def bank_d(p, kv, t):
        if t == 0:
            src, dst = (bk_ref, bv_ref)[kv].at[:, :, cols(p)], block(kv, y, p)
        elif t <= 2:
            src = dst = block(kv, y - (1 - 2 * (t - 1)), p)
        else:
            src = dst = half_block(kv, y + 2, t - 3, p)
        return remote(src, dst, d_s.at[p, kv, t], d_r.at[p, kv, t], sibling)

    def ag(s, k, h):
        before = 0 if k == 1 else s * 4 + k - 1
        return remote(
            qt.at[before, h], qt.at[s * 4 + k, h], g_s.at[s, k, h], g_r.at[s, k, h], dev_z(2 * s - 1)
        )

    def back(s, k, h):
        return (
            remote(rb.at[s, k, h], rb.at[s, k - 1, h], o_s.at[s, k, h], o_r.at[s, k - 1, h], dev_z(1 - 2 * s)),
            remote(lb.at[s, k, h], lb.at[s, k - 1, h], l_s.at[s, k, h], l_r.at[s, k - 1, h], dev_z(1 - 2 * s)),
        )

    def w_rows(xx, which, part=None):
        size = whalf if part is None else whalf // 2
        start = (xx + NX) % NX * wrows + which * whalf + (0 if part is None else part * size)
        return weight.at[pl.ds(pl.multiple_of(start, whalf // 2), size)]

    def w_x(d):
        return remote(
            w_ref.at[pl.ds(c * whalf, whalf)], w_rows(x, c), w_s.at[d], w_r.at[d], dev_x(1 if d == 0 else NX - 1)
        )

    def w_f(d):
        view = w_rows(x - (1 - 2 * d), c, d)
        return remote(view, view, wf_s.at[d], wf_r.at[d], dev_x(1 if d == 0 else NX - 1))

    def w_d(t):
        view = w_rows(x - (1 - 2 * t), c) if t < 2 else w_rows(x + 2, c)
        return remote(view, view, wd_s.at[t], wd_r.at[t], sibling)

    def attn_x(p, dx):
        peer = (x + dx) % NX
        return remote(
            mine.at[pl.ds(pl.multiple_of(peer * rows, rows), rows), cols(p)],
            arrived.at[:, lanes(x * width + p * 256, 256)],
            t_s.at[p, dx - 1], t_r.at[p, dx - 1], dev_x(dx),
        )

    def attn_own(p):
        return pltpu.make_async_copy(
            mine.at[my_rows, cols(p)], arrived.at[:, lanes(x * width + p * 256, 256)], t_own.at[p]
        )

    def w_mine():
        return pltpu.make_async_copy(w_ref, weight.at[pl.ds(pl.multiple_of(x * wrows, wrows), wrows)], w_own)

    def softmax(keys, values, queries, biases):
        scores = jnp.dot(keys, queries, preferred_element_type=jnp.float32) * factor
        if biases is not None:
            step = scores.shape[0] // len(biases)
            scores = jnp.concatenate(
                [scores[i * step : (i + 1) * step] + b for i, b in enumerate(biases)], axis=0
            )
        top = jnp.max(scores, axis=0, keepdims=True)
        expo = jnp.exp2(scores - top)
        total = jnp.sum(expo, axis=0, keepdims=True)
        numer = lax.dot_general(
            values, expo.astype(jnp.bfloat16), (((0,), (0,)), ((), ())),
            preferred_element_type=jnp.float32,
        )
        return numer / total, top + jnp.log2(total)

    def partial(p, odd, index, away):
        bank, h, where = banks[p], 2 * p + odd, (z + away + NZ) % NZ
        here = lanes(odd * HEAD_DIM, HEAD_DIM)
        listed = [table[where, i] for i in range(2 * PLANE)]
        picked = [jnp.maximum(r, 0) for r in listed]
        keys = jnp.concatenate([bank[0, r, :, here] for r in picked], axis=0)
        values = jnp.concatenate([bank[1, r, :, here] for r in picked], axis=0)
        biases = [jnp.where(r < 0, NEG, 0.0) for r in listed]
        return softmax(keys, values, qt[index, h], biases)

    def merge(a, b):
        (oa, la), (ob, lb_) = a, b
        top = jnp.maximum(la, lb_)
        wa, wb = jnp.exp2(la - top), jnp.exp2(lb_ - top)
        total = wa + wb
        return oa * (wa / total) + ob * (wb / total), top + jnp.log2(total)

    def put(s, k, h, part):
        rb[s, k, h] = part[0].astype(jnp.bfloat16)
        for i in range(4):
            lb[s, k, h, i : i + 1, :] = part[1][:, i * 128 : (i + 1) * 128]

    def get(s, k, h):
        lse = jnp.concatenate([lb[s, k, h, i : i + 1, :] for i in range(4)], axis=1)
        return rb[s, k, h].astype(jnp.float32), lse

    def plan():
        first = y * NZ * NC + c
        listed = picks_ref[pl.ds(first, NZ, stride=NC), :]
        span = lax.broadcasted_iota(jnp.int32, listed.shape, 0)
        position = lax.broadcasted_iota(jnp.int32, listed.shape, 1)
        number = jnp.zeros(listed.shape, jnp.int32)
        for i in range(NZ):
            number = jnp.where(span == i, counts_ref[first + i * NC], number)

        def look(i, found):
            for j in range(8):
                t = i * 8 + j
                found = jnp.where(listed == t, slot_ref[t], found)
            return found

        found = lax.fori_loop(0, slot_ref.shape[0] // 8, look, jnp.zeros(listed.shape, jnp.int32))
        magic = -(-65536 // frames)
        owner = (found * magic) >> 16
        here = (position < number) & (((owner >> 1) & (NZ - 1)) == z)
        holder = ((owner >> 4) << 1) + (owner & 1)
        place = holder * frames + found - owner * frames
        lane = lax.broadcasted_iota(jnp.int32, table_v.shape, 1)
        out = jnp.full(table_v.shape, -1, jnp.int32)
        for m in range(PLANE):
            mine_here = here & (holder == m)
            high = jnp.max(jnp.where(mine_here, place, -1), axis=1, keepdims=True)
            low = jnp.min(jnp.where(mine_here, place, 1 << 20), axis=1, keepdims=True)
            out = jnp.where(lane == 2 * m, high, out)
            out = jnp.where(lane == 2 * m + 1, jnp.where(low < high, low, -1), out)
        table_v[...] = out
        copy = pltpu.make_async_copy(table_v, table, table_sem)
        copy.start()
        copy.wait()

    def ag_step(p, k):
        for u in side_units(k):
            s, h = u // 2, 2 * p + u % 2
            if k > 1:
                ag(s, k - 1, h).wait_recv()
            ag(s, k, h).start()

    def ag_end(p):
        for u in range(4):
            s, h = u // 2, 2 * p + u % 2
            ag(s, 4 if (u // 2 + u % 2) % 2 == 0 else 3, h).wait_recv()

    def rs_step(p, j):
        units, stride = (4, 1) if j < 3 else (2, 3)

        def unit(i, carry):
            u = i * stride
            s = u // 2
            odd = u % 2
            h = 2 * p + odd
            k = 4 - (s + odd) % 2 - j
            part = partial(p, odd, s * 4 + k, k - 2 * s * k)
            if j:
                for copy in back(s, k + 1, h):
                    copy.wait_recv()
                part = merge(get(s, k, h), part)
            put(s, k, h, part)
            for copy in back(s, k, h):
                copy.start()
            return carry

        lax.fori_loop(0, units, unit, 0)

    def home_part(p):
        def one(i, carry):
            h = 2 * p + i
            here = lanes(h * HEAD_DIM, HEAD_DIM)
            part = merge(partial(p, i, 0, 0), softmax(kx[:, here], vx[:, here], qt[0, h], None))
            home[h] = part[0]
            hlse[h] = part[1]
            return carry

        lax.fori_loop(0, 2, one, 0)

    def finish(p):
        def one(i, carry):
            h = 2 * p + i
            here = lanes(h * HEAD_DIM, HEAD_DIM)
            part = (home[h], hlse[h])
            for s in range(2):
                for copy in back(s, 1, h):
                    copy.wait_recv()
                part = merge(part, get(s, 0, h))
            mine[:, here] = jnp.transpose(part[0]).astype(jnp.bfloat16)
            return carry

        lax.fori_loop(0, 2, one, 0)
        for dx in range(1, NX):
            attn_x(p, dx).start()
        attn_own(p).start()

    def w_ready():
        w_mine().wait()
        for t in range(3):
            w_d(t).wait_recv()

    def w_pass():
        for d in range(2):
            w_x(d).wait_recv()
            w_f(d).start()
            w_d(d).start()

    def w_last():
        for d in range(2):
            w_f(d).wait_recv()
        w_d(2).start()

    def project(p):
        for dx in range(1, NX):
            attn_x(p, dx).wait_recv()
        attn_own(p).wait()

        def columns(i, carry):
            here = pl.ds(pl.multiple_of(i * 512, 512), 512)
            part = acc[:, here] if p else 0.0
            for xx in range(NX):
                deep = pl.ds(xx * width + p * 256, 256)
                part = part + jnp.dot(arrived[:, deep], weight[deep, here], preferred_element_type=jnp.float32)
            if p == PAIRS - 1:
                out_ref[:, here] = part.astype(jnp.bfloat16)
            else:
                acc[:, here] = part
            return carry

        lax.fori_loop(0, out_ref.shape[1] // 512, columns, 0)

    def bank_start(p):
        for kv in range(2):
            for d in range(2):
                bank_a(p, kv, d).start()
            bank_d(p, kv, 0).start()

    def bank_pass(p):
        for kv in range(2):
            for d in range(2):
                bank_a(p, kv, d).wait_recv()
                bank_b(p, kv, d).start()
                bank_d(p, kv, 1 + d).start()

    def bank_last(p):
        for kv in range(2):
            for d in range(2):
                bank_b(p, kv, d).wait_recv()
                bank_d(p, kv, 3 + d).start()

    def bank_end(p):
        for kv in range(2):
            own_bank(kv, p).wait()
            for t in range(5):
                bank_d(p, kv, t).wait_recv()

    def load_queries(p):
        for dx in range(1, NX):
            x_query(p, dx).wait_recv()
        for h in (2 * p, 2 * p + 1):
            part = qx[:, h * HEAD_DIM : (h + 1) * HEAD_DIM]
            qt[0, h] = jnp.transpose(part.astype(jnp.float32)).astype(jnp.bfloat16)

    for i in range(3):
        own_rows(i).start()
    for p in range(PAIRS):
        for kv in range(2):
            own_bank(kv, p).start()
    barrier = pltpu.get_barrier_semaphore()
    for dev in (dev_x(1), dev_x(2), dev_x(3), sibling, dev_y(1), dev_y(-1), dev_z(1), dev_z(-1)):
        pl.semaphore_signal(barrier, inc=1, device_id=dev, device_id_type=MESH)
    pl.semaphore_wait(barrier, 8)

    for p in range(PAIRS):
        for dx in range(1, NX):
            x_query(p, dx).start()
    bank_start(0)
    own_rows(0).wait()
    load_queries(0)
    ag_step(0, 1)
    load_queries(1)
    ag_step(1, 1)
    load_queries(2)
    for kv in range(2):
        for dx in range(1, NX):
            x_keys(kv, dx).start()
    w_mine().start()
    for d in range(2):
        w_x(d).start()
    plan()
    ag_step(0, 2)
    ag_step(1, 2)
    bank_pass(0)
    bank_start(1)
    ag_step(0, 3)
    ag_step(1, 3)
    bank_last(0)
    ag_step(0, 4)
    ag_step(1, 4)
    ag_step(2, 1)
    bank_end(0)
    ag_end(0)
    rs_step(0, 0)
    ag_step(2, 2)
    bank_pass(1)
    bank_start(2)
    rs_step(0, 1)
    ag_step(2, 3)
    for i in (1, 2):
        own_rows(i).wait()
    for kv in range(2):
        for dx in range(1, NX):
            x_keys(kv, dx).wait_recv()
    home_part(0)
    bank_last(1)
    rs_step(0, 2)
    ag_step(2, 4)
    bank_end(1)
    ag_end(1)
    rs_step(1, 0)
    rs_step(0, 3)
    w_pass()
    bank_pass(2)
    ag_end(2)
    home_part(1)
    rs_step(1, 1)
    bank_last(2)
    bank_end(2)
    rs_step(2, 0)
    finish(0)
    rs_step(1, 2)
    rs_step(2, 1)
    home_part(2)
    w_last()
    rs_step(1, 3)
    rs_step(2, 2)
    finish(1)
    rs_step(2, 3)
    finish(2)
    w_ready()
    project(0)
    project(1)
    project(2)

    for p in range(PAIRS):
        for dx in range(1, NX):
            x_query(p, dx).wait_send()
            attn_x(p, dx).wait_send()
        for kv in range(2):
            for d in range(2):
                bank_a(p, kv, d).wait_send()
                bank_b(p, kv, d).wait_send()
            for t in range(5):
                bank_d(p, kv, t).wait_send()
        for k in range(1, 5):
            for u in side_units(k):
                s, h = u // 2, 2 * p + u % 2
                ag(s, k, h).wait_send()
                for copy in back(s, k, h):
                    copy.wait_send()
    for dx in range(1, NX):
        for kv in range(2):
            x_keys(kv, dx).wait_send()
    for d in range(2):
        w_x(d).wait_send()
        w_f(d).wait_send()
    for t in range(3):
        w_d(t).wait_send()


def local(span_q, span_k, span_v, bank_k, bank_v, frame_slot, picks, counts, out_weight):
    width = bank_k.shape[2]
    heads = width // HEAD_DIM
    span_rows = span_q.shape[0] * NX
    model = span_q.shape[1]
    bf, dma = jnp.bfloat16, pltpu.SemaphoreType.DMA
    smem = pl.BlockSpec(memory_space=pltpu.SMEM)
    hbm = pl.BlockSpec(memory_space=pl.ANY)
    return pl.pallas_call(
        kernel,
        out_shape=jax.ShapeDtypeStruct((span_q.shape[0], out_weight.shape[1]), bf),
        in_specs=[pl.BlockSpec(memory_space=pltpu.VMEM), smem, smem] + [hbm] * 6,
        out_specs=pl.BlockSpec(memory_space=pltpu.VMEM),
        scratch_shapes=[
            pltpu.VMEM((span_rows, width), bf),
            pltpu.VMEM((span_rows, width), bf),
            pltpu.VMEM((span_rows, width), bf),
            *[pltpu.VMEM((2, PLANE * bank_k.shape[0], bank_k.shape[1], 256), bf)] * PAIRS,
            pltpu.VMEM((9, heads, HEAD_DIM, span_rows), bf),
            pltpu.VMEM((2, 5, heads, HEAD_DIM, span_rows), bf),
            pltpu.VMEM((2, 5, heads, 4, 128), jnp.float32),
            pltpu.VMEM((heads, HEAD_DIM, span_rows), jnp.float32),
            pltpu.VMEM((heads, 1, span_rows), jnp.float32),
            pltpu.VMEM((span_q.shape[0], model), bf),
            pltpu.VMEM((model, out_weight.shape[1]), bf),
            pltpu.VMEM((span_q.shape[0], out_weight.shape[1]), jnp.float32),
            pltpu.VMEM((NZ, 128), jnp.int32),
            pltpu.SMEM((NZ, 128), jnp.int32),
            dma((PAIRS, NX - 1)), dma((PAIRS, NX - 1)),
            dma((2, NX - 1)), dma((2, NX - 1)),
            dma((3,)), dma((PAIRS, 2)),
            dma((2,)), dma((2,)), dma((2,)), dma((2,)), dma((3,)), dma((3,)),
            dma((PAIRS, 2, 2)), dma((PAIRS, 2, 2)),
            dma((PAIRS, 2, 2)), dma((PAIRS, 2, 2)),
            dma((PAIRS, 2, 5)), dma((PAIRS, 2, 5)),
            dma((2, 5, heads)), dma((2, 5, heads)),
            dma((2, 5, heads)), dma((2, 5, heads)),
            dma((2, 5, heads)), dma((2, 5, heads)),
            dma((PAIRS, NX - 1)), dma((PAIRS, NX - 1)), dma((PAIRS,)), dma(()), dma(()),
        ],
        compiler_params=pltpu.CompilerParams(
            collective_id=0, has_side_effects=True, vmem_limit_bytes=63 * 2**20
        ),
    )(picks, counts, frame_slot, span_q, span_k, span_v, bank_k, bank_v, out_weight)


def solution(mesh):
    placed = (
        P(("frame", "head"), None),
        P(("frame", "head"), None),
        P(("frame", "head"), None),
        P("frame", None, "head"),
        P("frame", None, "head"),
        P(),
        P(),
        P(),
        P("head", None),
    )
    return jax.shard_map(
        local, mesh=mesh, in_specs=placed, out_specs=P(("frame", "head"), None), check_vma=False
    )
```
